32 devices in a mesh: groups: 2 (over x), section: 16 (over z, y, core).
Axes of the slice: x: 2, y: 2, z: 4, core: 2. Of those that a mesh axis runs over, the one named last changes fastest.
Arguments:
- queries: bfloat16 [4096, 4096], P(('groups', 'section')), parts along dimension 0, may hold values from -400 to 400
- keys: bfloat16 [4096, 256], P(('groups', 'section')), parts along dimension 0, may hold values from -4 to 4
- values: bfloat16 [4096, 256], P(('groups', 'section')), parts along dimension 0, may hold values from -6 to 6
- windows: int32 [32], P('groups'), parts along dimension 0, may hold values from 0 to 1024, as said below
Outputs:
- attended: bfloat16 [4096, 4096], P(('groups', 'section')), parts along dimension 0
- log_total: float32 [4096, 32], P(('groups', 'section')), parts along dimension 0
The draws below stay inside these ranges and needn't reach their ends.
There are 2 independent parts, one for each index of `groups`. The reference program is written for one: setup_inputs(seed, part) draws one part's arguments, and reference() takes and returns one part's arrays. A program takes and returns all parts, laid end to end along the dimension named above; each array names one. Nothing has to cross between parts.
Inputs may be any that keep to these rules, and one draw needn't show every extreme that they name: `windows`: the first slice's window is 0 and the last slice's window is 1024.
All inputs are finite; a program needn't handle non-finite values.
Results may differ from the reference program's by a relative error of at most 0.0055.
Values may be sent and summed in bfloat16 or wider, within the bound.
A program may use at most 64 MiB of HBM per device.

```python
import jax
import jax.numpy as jnp
from jax import lax

QH = 32
KVH = 2
HD = 128
SR = 128
WMAX = 1024
S = 2048
N_SECTION = 16


def make_pair(key):
    token_count = SR * N_SECTION
    key_q = jax.random.fold_in(key, 101)
    key_k = jax.random.fold_in(key, 102)
    base_q = jnp.clip(jax.random.normal(key_q, (token_count, QH, HD), jnp.float32), -4.0, 4.0)
    base_k = jnp.clip(jax.random.normal(key_k, (token_count, KVH, HD), jnp.float32), -4.0, 4.0)
    return (base_q.reshape(token_count, QH * HD), base_k.reshape(token_count, KVH * HD))


def draw_queries(key, part):
    return make_pair(key)[0].astype(jnp.bfloat16)


def draw_keys(key, part):
    return make_pair(key)[1].astype(jnp.bfloat16)


def draw_windows(key, part):
    key_base = jax.random.fold_in(key, 201)
    key_full = jax.random.fold_in(key, 202)
    base = jax.random.randint(key_base, (N_SECTION,), 0, WMAX + 1)
    full = jax.random.randint(key_full, (N_SECTION,), 0, 4) == 0
    position = jnp.arange(N_SECTION)
    full = full | (position == N_SECTION - 1)
    chosen = jnp.where(full, WMAX, base)
    chosen = jnp.where(position == 0, 0, chosen)
    return chosen.astype(jnp.int32)


def level_of(key, extent, split, low, top_value):
    gain = 1.0
    for dim, blocks in split:
        draws = jax.random.uniform(jax.random.fold_in(jax.random.fold_in(key, 6), dim), (blocks,), jnp.float32, low / len(split), top_value / len(split))
        gain = gain * jnp.repeat(jnp.exp(draws), extent[dim] // blocks).reshape((-1,) + (1,) * (len(extent) - 1 - dim))
    return gain


def normal_values(stream_key, dims, width, most, split=(), kind=jnp.bfloat16):
    entries = width * jax.random.normal(stream_key, dims, jnp.float32)
    if split:
        entries = entries * level_of(stream_key, dims, split, -0.22, 0.18)
    return jnp.clip(entries, -most, most).astype(kind)


def setup_inputs(seed: int = 0, part: int = 0) -> dict:
    streams_of = jax.random.split(jax.random.key(seed), 5)
    own_keys = jax.random.split(jax.random.fold_in(streams_of[4], part), 5)
    return {
        "queries": draw_queries(jax.random.fold_in(jax.random.fold_in(streams_of[4], part), 71), part),
        "keys": draw_keys(jax.random.fold_in(jax.random.fold_in(streams_of[4], part), 71), part),
        "values": normal_values(own_keys[2], (S, KVH * HD), 1.0, 6.0, ((0, 16),)),
        "windows": draw_windows(jax.random.fold_in(jax.random.fold_in(streams_of[4], part), 71), part),
    }


def reference(queries, keys, values, windows):
    per_group = QH // KVH
    scale = HD ** -0.5
    span = WMAX + SR
    padded_keys = jnp.concatenate([jnp.zeros((WMAX, KVH * HD), keys.dtype), keys], 0)
    padded_values = jnp.concatenate([jnp.zeros((WMAX, KVH * HD), values.dtype), values], 0)

    def one_slice(index):
        row_start = (index * SR).astype(jnp.int32)
        block_q = lax.dynamic_slice_in_dim(queries, row_start, SR, 0).reshape(SR, KVH, per_group, HD).astype(jnp.float32)
        block_k = lax.dynamic_slice_in_dim(padded_keys, row_start, span, 0).reshape(span, KVH, HD).astype(jnp.float32)
        block_v = lax.dynamic_slice_in_dim(padded_values, row_start, span, 0).reshape(span, KVH, HD).astype(jnp.float32)
        scores = jnp.einsum('rgjd,ngd->gjrn', block_q, block_k) * scale
        key_pos = row_start - WMAX + jnp.arange(span, dtype=jnp.int32)
        row_pos = row_start + jnp.arange(SR, dtype=jnp.int32)
        lowest = row_start - windows[index]
        visible = (key_pos[None, :] >= lowest) & (key_pos[None, :] >= 0) & (key_pos[None, :] <= row_pos[:, None])
        scores = jnp.where(visible, scores, jnp.float32(-1e30))
        row_max = jnp.max(scores, -1)
        expos = jnp.where(visible, jnp.exp(scores - row_max[..., None]), jnp.float32(0.0))
        total = jnp.sum(expos, -1)
        rounded = lax.optimization_barrier(expos.astype(jnp.bfloat16)).astype(jnp.float32)
        summed = jnp.einsum('gjrn,ngd->rgjd', rounded, block_v)
        output = (summed / jnp.transpose(total, (2, 0, 1))[..., None]).reshape(SR, QH * HD).astype(jnp.bfloat16)
        log_sum = jnp.transpose(row_max + jnp.log(total), (2, 0, 1)).reshape(SR, QH)
        return output, log_sum

    outputs, log_sums = lax.map(one_slice, jnp.arange(N_SECTION, dtype=jnp.int32))
    return outputs.reshape(N_SECTION * SR, QH * HD), log_sums.reshape(N_SECTION * SR, QH)
```

```python
import functools

import jax
import jax.numpy as jnp
from jax import lax
from jax.experimental import pallas as pl
from jax.experimental.pallas import tpu as pltpu
from jax.sharding import PartitionSpec as P

HD = 128
PLANE = 4
BATCH = 16
SPLIT = 2
PIECES = 2 * SPLIT
ONES = 16
CHUNK = 4
CAST_FIRST = True
LOG2E = 1.4426950408889634
LN2 = 0.6931471805599453
SCALE2 = HD ** (-0.5) * LOG2E
CONTRACT_LAST = (((1,), (1,)), ((), ()))


def kernel(
    section,
    q_hbm,
    k_hbm,
    v_hbm,
    windows,
    acc,
    top,
    q,
    slots,
    kx,
    vt,
    local_sem,
    send_sem,
    recv_sem,
):
    reach = section // 2
    rows = q.shape[0]
    kv_heads = kx.shape[0]
    heads = q.shape[1] // HD
    per_group = heads // kv_heads
    batch = BATCH
    me = lax.axis_index("section")
    z, y, c = me // PLANE, (me // 2) % 2, me % 2
    last_z = section // PLANE - 1

    q_in = pltpu.make_async_copy(q_hbm, q, local_sem.at[0])
    k_in = pltpu.make_async_copy(k_hbm, slots.at[0, 0], local_sem.at[1])
    v_in = pltpu.make_async_copy(v_hbm, slots.at[0, 1], local_sem.at[2])
    k_in.start()
    v_in.start()
    q_in.start()

    barrier = pltpu.get_barrier_semaphore()

    def greet(other):
        pl.semaphore_signal(barrier, inc=1, device_id={"section": other})

    greet(me + 1 - 2 * c)
    greet(me + 2 - 4 * y)
    pl.when(z < last_z)(lambda: greet(me + PLANE))
    pl.when(z > 0)(lambda: greet(me - PLANE))
    pl.semaphore_wait(
        barrier, 2 + (z < last_z).astype(jnp.int32) + (z > 0).astype(jnp.int32)
    )

    def sends(slot):
        found = []
        if slot % PLANE == 0:
            if slot + PLANE <= reach:
                found.append((z < last_z, slot + PLANE, me + PLANE, 0))
            if slot + 2 <= reach:
                found.append((y == 0, slot + 2, me + 2, 1))
            if slot >= 2:
                found.append((y == 1, slot - 2, me - 2, 1))
        if slot + 1 <= reach:
            found.append((c == 0, slot + 1, me + 1, 2))
        if slot >= 1:
            found.append((c == 1, slot - 1, me - 1, 2))
        return found

    def piece_rows(piece):
        size = rows // SPLIT
        return pl.ds(piece % SPLIT * size, size)

    def describe(slot, piece, target, other, kind):
        kind_of, part = piece // SPLIT, piece_rows(piece)
        if slot:
            source = slots.at[slot, kind_of, part]
        else:
            source = (k_hbm, v_hbm)[kind_of].at[part]
        return pltpu.make_async_remote_copy(
            src_ref=source,
            dst_ref=slots.at[target, kind_of, part],
            send_sem=send_sem.at[slot // 2, kind, piece],
            recv_sem=recv_sem.at[target, piece],
            device_id={"section": other},
        )

    def relay(slot, piece):
        for condition, target, other, kind in sends(slot):
            copy = describe(slot, piece, target, other, kind)
            pl.when(condition & (me >= slot))(copy.start)

    def finish(slot, piece):
        for condition, target, other, kind in sends(slot):
            copy = describe(slot, piece, target, other, kind)
            pl.when(condition & (me >= slot))(copy.wait_send)

    def arrive(slot, piece):
        copy = pltpu.make_async_remote_copy(
            src_ref=slots.at[slot, piece // SPLIT, piece_rows(piece)],
            dst_ref=slots.at[slot, piece // SPLIT, piece_rows(piece)],
            send_sem=send_sem.at[0, 0, piece],
            recv_sem=recv_sem.at[slot, piece],
            device_id={"section": me},
        )
        pl.when(me >= slot)(copy.wait_recv)

    window = windows[me]
    takes, groups, rest = [[PLANE]], [[PLANE]], [1, 2, 3]
    for far in range(2 * PLANE, reach + 1, PLANE):
        takes += [[far - PLANE - 2, far] if far == 2 * PLANE else [far], [far - 2]]
        groups += [rest, [far - 1, far]]
        rest = [far - 3, far - 2]
    takes.append([])
    groups.append(rest)
    place = {0: 0}
    for group in groups:
        for slot in group:
            place[slot] = len(place)

    def actual(label):
        if label < PLANE or label % 2 == 0:
            return label
        return label - 2 * c if label % PLANE == 3 else label + 2 * c

    def prepare(label):
        slot = actual(label)
        ages = slot * rows - lax.broadcasted_iota(jnp.int32, (rows, HD), 0)
        seen = (ages <= window) & (me >= slot)
        lane_ages = slot * rows - lax.broadcasted_iota(jnp.int32, (ONES, rows), 1)
        lane_seen = (lane_ages <= window) & (me >= slot)
        span = slice(place[label] * rows, (place[label] + 1) * rows)
        for g in range(kv_heads):
            cols = slice(g * HD, (g + 1) * HD)
            key = slots[slot, 0, :, cols].astype(jnp.float32)
            value = slots[slot, 1, :, cols].astype(jnp.float32)
            if label:
                spare = slots[0, 0, 0:1, cols].astype(jnp.float32)
                key = jnp.where(seen, key, spare)
                value = jnp.where(seen, value, 0.0)
            scaled = key * SCALE2
            high = scaled.astype(jnp.bfloat16)
            low = (scaled - high.astype(jnp.float32)).astype(jnp.bfloat16)
            kx[g, span, 0:HD] = high
            kx[g, span, HD : 2 * HD] = low
            vt[g, 0:HD, span] = value.T.astype(jnp.bfloat16)
            if label:
                counted = jnp.where(lane_seen, 1.0, 0.0)
            else:
                counted = jnp.ones((ONES, rows), jnp.float32)
            vt[g, HD : HD + ONES, span] = counted.astype(jnp.bfloat16)

    def attend(begin, count, first, last):
        span = slice(begin * rows, (begin + count) * rows)
        for number in range(heads // batch):
            g = number * batch // per_group
            columns = [
                slice((number * batch + j) * HD, (number * batch + j + 1) * HD)
                for j in range(batch)
            ]
            stacked = jnp.concatenate([q[:, col] for col in columns], 0)
            doubled = jnp.concatenate([stacked, stacked], 1)
            scores = lax.dot_general(
                kx[g, span, :],
                doubled,
                CONTRACT_LAST,
                preferred_element_type=jnp.float32,
            )
            if first:
                key_pos = lax.broadcasted_iota(jnp.int32, (rows, rows), 0)
                row_pos = lax.broadcasted_iota(jnp.int32, (rows, rows), 1)
                causal = jnp.concatenate([key_pos <= row_pos] * batch, 1)
                scores = jnp.where(causal, scores, -1e30)
            highest = jnp.max(scores, 0, keepdims=True)
            if not first:
                before = top[number]
                highest = jnp.maximum(highest, before)
                factor = jnp.exp2(before - highest)
            weights = jnp.exp2(scores - highest).astype(jnp.bfloat16)
            update = jnp.dot(
                vt[g, :, span], weights, preferred_element_type=jnp.float32
            )
            summed = update[0 : HD + 8]
            if not first:
                summed = summed + acc[number] * factor
            top[number] = highest
            acc[number] = summed

    def take(label):
        slot = actual(label)
        for piece in range(PIECES):
            arrive(slot, piece)
            if label % 2 == 0:
                relay(slot, piece)

    def absorb(group, last=False):
        for slot in group:
            if slot % 2:
                take(slot)
            prepare(slot)
        attend(place[group[0]], len(group), False, last)

    for piece in range(PIECES):
        relay(0, piece)
    k_in.wait()
    v_in.wait()
    prepare(0)
    q_in.wait()
    attend(0, 1, True, False)
    for number, group in enumerate(groups):
        for slot in takes[number]:
            take(slot)
        absorb(group, number == len(groups) - 1)
    for slot in range(0, reach + 1, 2):
        for piece in range(PIECES):
            finish(slot, piece)


def finish_kernel(acc, top, attended, log_total, staged, level, sems):
    batches = acc.shape[0]
    copies = []
    for number in range(batches):
        for part in range(BATCH // CHUNK):
            span = slice(part * CHUNK * HD, (part + 1) * CHUNK * HD)
            total = acc[number, HD : HD + 1, span]
            inverse = 1.0 / total
            levels = top[number, :, span] * LN2 + jnp.log(total)
            for j in range(CHUNK):
                head = number * BATCH + part * CHUNK + j
                side = slice((part * CHUNK + j) * HD, (part * CHUNK + j + 1) * HD)
                here = slice(j * HD, (j + 1) * HD)
                result = acc[number, 0:HD, side] * inverse[:, here]
                staged[:, head * HD : (head + 1) * HD] = result.astype(jnp.bfloat16).T if CAST_FIRST else result.T.astype(jnp.bfloat16)
                level[head : head + 1, :] = levels[:, here]
            first = number * BATCH + part * CHUNK
            cols = pl.ds(first * HD, CHUNK * HD)
            copy = pltpu.make_async_copy(staged.at[:, cols], attended.at[:, cols], sems.at[len(copies)])
            copy.start()
            copies.append(copy)
    copy = pltpu.make_async_copy(level, log_total, sems.at[len(copies)])
    copy.start()
    copies.append(copy)
    for copy in copies:
        copy.wait()


def solution(mesh):
    section = mesh.shape["section"]
    reach = section // 2

    def on_device(queries, keys, values, windows):
        rows = queries.shape[0]
        heads = queries.shape[1] // HD
        kv_heads = keys.shape[1] // HD
        batches = heads // BATCH
        length = (reach + 1) * rows
        acc, top = pl.pallas_call(
            functools.partial(kernel, section),
            out_shape=(
                pltpu.VMEM((batches, HD + 8, BATCH * rows), jnp.float32),
                pltpu.VMEM((batches, 1, BATCH * rows), jnp.float32),
            ),
            in_specs=[pl.BlockSpec(memory_space=pl.ANY)] * 3
            + [pl.BlockSpec(memory_space=pltpu.SMEM)],
            out_specs=(
                pl.BlockSpec(memory_space=pltpu.VMEM),
                pl.BlockSpec(memory_space=pltpu.VMEM),
            ),
            scratch_shapes=[
                pltpu.VMEM(queries.shape, jnp.bfloat16),
                pltpu.VMEM((reach + 1, 2) + keys.shape, jnp.bfloat16),
                pltpu.VMEM((kv_heads, length, 2 * HD), jnp.bfloat16),
                pltpu.VMEM((kv_heads, HD + ONES, length), jnp.bfloat16),
                pltpu.SemaphoreType.DMA((3,)),
                pltpu.SemaphoreType.DMA((reach // 2 + 1, 3, PIECES)),
                pltpu.SemaphoreType.DMA((reach + 1, PIECES)),
            ],
            compiler_params=pltpu.CompilerParams(
                collective_id=0, has_side_effects=True
            ),
        )(queries, keys, values, windows)
        acc = pltpu.with_memory_space_constraint(acc, pltpu.VMEM)
        top = pltpu.with_memory_space_constraint(top, pltpu.VMEM)
        attended, log_total = pl.pallas_call(
            finish_kernel,
            out_shape=(
                jax.ShapeDtypeStruct(queries.shape, jnp.bfloat16),
                jax.ShapeDtypeStruct((heads, rows), jnp.float32),
            ),
            in_specs=[pl.BlockSpec(memory_space=pltpu.VMEM)] * 2,
            out_specs=(
                pl.BlockSpec(memory_space=pl.ANY),
                pl.BlockSpec(memory_space=pl.ANY),
            ),
            scratch_shapes=[
                pltpu.VMEM(queries.shape, jnp.bfloat16),
                pltpu.VMEM((heads, rows), jnp.float32),
                pltpu.SemaphoreType.DMA((heads // CHUNK + 1,)),
            ],
            compiler_params=pltpu.CompilerParams(vmem_limit_bytes=16 * 2**20),
        )(acc, top)
        return attended, log_total.T

    placed = (
        P(("groups", "section"), None),
        P(("groups", "section"), None),
        P(("groups", "section"), None),
        P("groups"),
    )
    return jax.shard_map(
        on_device,
        mesh=mesh,
        in_specs=placed,
        out_specs=(P(("groups", "section"), None), P(("groups", "section"), None)),
        check_vma=False,
    )
```
